512 devices in a mesh: row: 32 (over z_lo, x, core), col: 16 (over z_hi, y).
Axes of the slice: x: 4, y: 8, z: 8 (z_hi: 2, z_lo: 4; z = z_hi * 4 + z_lo), core: 2. Of those that a mesh axis runs over, the one named last changes fastest.
Arguments:
- state: float32 [32, 2, 16, 256, 256], P('row', None, 'col'), may hold values from -6 to 6
- a_tiles: float32 [32, 2, 16, 256, 256], P('row', None, 'col'), may hold values from -0.375 to 0.375
- inverses: float32 [32, 256, 256], P('row'), may hold values from -0.225 to 1.025
Outputs:
- state_out: float32 [32, 2, 16, 256, 256], P('row', None, 'col')
The draws below stay inside these ranges and needn't reach their ends.
All inputs are finite; a program needn't handle non-finite values.
Results may differ from the reference program's by a relative error of at most 0.0001.
Values sent between devices are 32-bit elements; how exact they have to be, the bound alone decides.
A program may use at most 64 MiB of HBM per device.

```python
import math
import jax
import jax.numpy as jnp
from jax import lax

B = 256
FRONTS = 3
DOUBLINGS = 5
NT = 32
CW = 2
N_COL = 16


def draw_inverses(key, part):
    own_key = jax.random.fold_in(key, 11)
    noise = jax.random.normal(own_key, (NT, B, B), jnp.float32)
    noise = jnp.clip(noise, -6.0, 6.0)
    return 0.8 * jnp.eye(B, dtype=jnp.float32)[None] - 0.6 / math.sqrt(B) * noise


def block_scale(stream_key, extent, shards, least, high):
    level, own = 1.0, jax.random.fold_in(stream_key, 6)
    for position, parts in shards:
        steps = jnp.exp(jax.random.uniform(jax.random.fold_in(own, position), (parts,), jnp.float32, least / len(shards), high / len(shards)))
        level = level * jnp.repeat(steps, extent[position] // parts).reshape([-1 if axis == position else 1 for axis in range(len(extent))])
    return level


def bell_draw(key, extent, deviation, bound, pieces=(), kind=jnp.bfloat16):
    drawn = jax.random.normal(key, extent, jnp.float32) * deviation
    if len(pieces) > 0:
        drawn = block_scale(key, extent, pieces, -0.22, 0.18) * drawn
    return jnp.clip(drawn, min=-bound, max=bound).astype(kind)


def setup_inputs(seed: int = 0) -> dict:
    key_list = jax.random.split(jax.random.key(seed), 4)
    return {
        "state": bell_draw(key_list[0], (NT, CW, N_COL, B, B), 1.0, 6.0, ((0, 32), (2, 16)), jnp.float32),
        "a_tiles": bell_draw(key_list[1], (NT, CW, N_COL, B, B), B ** -0.5, 0.375, ((0, 32), (2, 16)), jnp.float32),
        "inverses": draw_inverses(jax.random.fold_in(key_list[3], 71), 0),
    }


HIGH = lax.Precision.HIGHEST
shift_half = 0.5


def batched_product(left, right):
    return jnp.einsum("nab,nbc->nac", left, right, precision=HIGH, preferred_element_type=jnp.float32)


def batched_transposed(left, right):
    return jnp.einsum("nab,ncb->nac", left, right, precision=HIGH, preferred_element_type=jnp.float32)


def reference(state, a_tiles, inverses):
    tile_grid = state.reshape(NT, NT, B, B)
    coupling = a_tiles.reshape(NT, NT, B, B)
    identity_tile = jnp.eye(B, dtype=jnp.float32)
    left_powers = [identity_tile[None] - shift_half * inverses]
    for level in range(DOUBLINGS - 1):
        left_powers.append(batched_product(left_powers[-1], left_powers[-1]))
    row_ids = jnp.arange(NT, dtype=jnp.int32)
    tile_sum = row_ids[:, None] + row_ids[None, :]
    for front_step in range(FRONTS):
        front_sum = NT - 1 - front_step
        partner = front_sum - row_ids
        partner_safe = jnp.clip(partner, 0, NT - 1).astype(jnp.int32)
        own_tiles = tile_grid[row_ids, partner_safe]
        far_tiles = tile_grid[partner_safe, row_ids]
        right_side = own_tiles + jnp.swapaxes(far_tiles, 1, 2)
        right_inverse = inverses[partner_safe]
        solution = shift_half * batched_transposed(batched_product(inverses, right_side), right_inverse)
        for level in range(DOUBLINGS):
            right_power = left_powers[level][partner_safe]
            solution = solution + batched_transposed(batched_product(left_powers[level], solution), right_power)
        passed = solution[partner_safe]

        def row_update(row_tiles):
            return batched_product(row_tiles[partner_safe], passed)

        updates = lax.map(row_update, coupling)
        shrink = (tile_sum < front_sum)[:, :, None, None]
        place = (tile_sum == front_sum)[:, :, None, None]
        tile_grid = jnp.where(shrink, tile_grid - updates, jnp.where(place, solution[:, None], tile_grid))
    return tile_grid.reshape(NT, CW, NT // CW, B, B)
```

```python
import functools

import jax
import jax.numpy as jnp
from jax import lax
from jax.experimental import pallas as pl
from jax.experimental.pallas import tpu as pltpu
from jax.sharding import PartitionSpec as P

FRONTS = 3
DOUBLINGS = 5
X_CHIPS = 4
F32 = jnp.float32
BF16 = jnp.bfloat16
MESH = pl.DeviceIdType.MESH


def split(value):
    high = value.astype(BF16)
    low = (value - high.astype(F32)).astype(BF16)
    return high, low


def dot(left, right):
    return jnp.dot(left, right, preferred_element_type=F32)


def product(left, right):
    return dot(left[0], right[0]) + (dot(left[0], right[1]) + dot(left[1], right[0]))


class Posted:
    def __init__(self, sems):
        self.sems = sems
        self.items = []

    def send(self, condition, src, dst, recv_sem, row, col):
        copy = pltpu.make_async_remote_copy(
            src_ref=src, dst_ref=dst, send_sem=self.sems.at[len(self.items)],
            recv_sem=recv_sem, device_id=(row, col), device_id_type=MESH,
        )
        self.items.append((condition, copy))

        @pl.when(condition)
        def _():
            copy.start()

    def drain(self):
        for condition, copy in self.items:
            @pl.when(condition)
            def _():
                copy.wait_send()


def landed(ref, sem):
    pltpu.make_async_copy(ref, ref, sem).wait()


N_SENDS = 192


def sweep(nt, nc, nx, state, coupling, inverse, out,
          flip, wide, inv_far, h_far, a_far, x_near, own, acc,
          left_hi, left_lo, right_hi, right_lo, tmp_hi, tmp_lo,
          send_sems, flip_sems, wide_sems, far_sems, near_sems):
    order = inverse.shape[-1]
    piece = order // nx
    per_plane = 2 * nx
    planes = nt // per_plane
    row, col = lax.axis_index("row"), lax.axis_index("col")
    plane, chip, core = row // per_plane, (row // 2) % nx, row % 2
    posted = Posted(send_sems)
    last = nt - 1
    lag = last - col - row
    role = [(lag == s) | (lag == s + nc) for s in range(FRONTS)]
    slot = jnp.where(lag >= nc, 1, 0)
    lags = [lag, lag - nc]

    def source_row(s, t):
        return last - s - nc * t - col

    for s in range(FRONTS):
        other = last - s - row
        posted.send(role[s] & (other != row), state.at[slot], h_far, far_sems.at[0], other, row % nc)
        posted.send((col == row % nc) & (other >= 0) & (other != row),
                    inverse, inv_far, far_sems.at[1], other, col)
        for step in range(1, s + 1):
            posted.send((col == (row + step) % nc) & (other >= 0) & (row + step <= last),
                        coupling.at[(row + step) // nc % 2], a_far.at[step - 1], far_sems.at[1 + step],
                        other, row % nc)

    for u in range(2):
        used = nc * u + col > row
        posted.send(used & (col != nc - 1) & (2 * col != nc - 2), coupling.at[u], flip.at[1, 1 - u],
                    flip_sems.at[1, 1 - u], row, nc - 2 - col)
    posted.send((col == nc - 1) & (last > row), coupling.at[1], flip.at[0, 0], flip_sems.at[0, 0], row, 0)
    for u in range(2):
        @pl.when((nc * u + col > row) & (2 * col == nc - 2))
        def _():
            flip[1, 1 - u] = coupling[u]

    @pl.when((nc - 1 > row) & (col == nc - 1))
    def _():
        flip[1, 0] = coupling[0]

    solver = role[0] | role[1] | role[2]
    flip_local = (2 * col == nc - 2) | (col == nc - 1)

    def hand_on(early):
        now = ~role[0] if early else role[0]
        for t in range(2):
            held = source_row(1, t) > row

            @pl.when(now & held & ~flip_local)
            def _():
                landed(flip.at[1, t], flip_sems.at[1, t])
            up = t + jnp.where(col == nc - 1, 1, 0)
            posted.send(now & held, flip.at[1, t], flip.at[0, up % 2], flip_sems.at[0, up % 2],
                        row, (col + 1) % nc)
            down = t - jnp.where(col == 0, 1, 0)
            posted.send(now & held & (down >= 0), flip.at[1, t], flip.at[2, down % 2],
                        flip_sems.at[2, down % 2], row, (col + nc - 1) % nc)

    hand_on(True)

    eye = (lax.broadcasted_iota(jnp.int32, (order, order), 0)
           == lax.broadcasted_iota(jnp.int32, (order, order), 1)).astype(F32)

    def powers(first, high, low):
        acc[...] = first

        def step(m, carry):
            value = split(acc[...])
            high[m], low[m] = value
            acc[...] = product(value, value)
            return carry
        lax.fori_loop(0, DOUBLINGS - 1, step, 0)
        high[DOUBLINGS - 1], low[DOUBLINGS - 1] = split(acc[...])

    self_mirror = role[1] & (2 * row == last - 1)
    mirrored = solver & ~self_mirror

    @pl.when(solver)
    def _():
        powers(eye - 0.5 * inverse[...], left_hi, left_lo)

        @pl.when(mirrored)
        def _():
            landed(inv_far, far_sems.at[1])

        @pl.when(self_mirror)
        def _():
            inv_far[...] = inverse[...]
            h_far[...] = state[slot]
        inv_far[...] = inv_far[...].T
        powers(eye - 0.5 * inv_far[...], right_hi, right_lo)

        @pl.when(mirrored)
        def _():
            landed(h_far, far_sems.at[0])
        acc[...] = state[slot] + h_far[...].T

    def transposed(ref):
        return split(ref[...].T)

    def solve():
        first = product(split(inverse[...]), split(acc[...]))
        own[...] = 0.5 * product(split(first), split(inv_far[...]))

        def level(m, carry):
            value = own[...]
            middle = product((left_hi[m], left_lo[m]), split(value))
            own[...] = value + product(split(middle), (right_hi[m], right_lo[m]))
            return carry
        lax.fori_loop(0, DOUBLINGS, level, 0)

    def spread(s):
        mirror = last - s - row
        for step in range(1, FRONTS - s):
            spot = 2 * (step - 1)
            if s + step == 2 and step == 1:
                spot = 0
            posted.send(role[s] & (row >= step), own, x_near.at[spot], near_sems.at[spot], row - step, col)
            posted.send(role[s] & (mirror >= step), own, x_near.at[spot + 1], near_sems.at[spot + 1],
                        row, (col + nc - step) % nc)
        for q in range(nx):
            posted.send(role[s] & (row >= 1) & (chip != q), own.at[pl.ds(q * piece, piece)],
                        wide.at[s, slot, pl.ds(q * piece, piece)], wide_sems.at[s, slot, q],
                        plane * per_plane + 2 * q + core, col)

    def relay(s):
        for t in range(2):
            src = source_row(s, t)
            top_plane, top_chip, side = src // per_plane, (src // 2) % nx, src % 2
            live = src >= 1
            here = live & (core == side)
            source = here & (row == src)
            level = here & (plane == top_plane)
            below = here & (plane < top_plane)
            span = pl.ds(pl.multiple_of(chip * piece, 8), piece)
            mine = wide.at[s, t, span]
            own_part = own.at[span]

            @pl.when((level & ~source) | below)
            def _():
                landed(mine, wide_sems.at[s, t, chip])
            for target in range(planes - 1):
                go = level & (target < top_plane)
                dst_row = target * per_plane + 2 * chip + core
                posted.send(go & ~source, mine, mine, wide_sems.at[s, t, chip], dst_row, col)
                posted.send(go & source, own_part, mine, wide_sems.at[s, t, chip], dst_row, col)
            for q in range(nx):
                go = (chip != q) & (below | (level & (q < top_chip)))
                dst_row = plane * per_plane + 2 * q + core
                posted.send(go & ~source, mine, mine, wide_sems.at[s, t, chip], dst_row, col)
                posted.send(go & source, own_part, mine, wide_sems.at[s, t, chip], dst_row, col)
            full = below | (level & (chip < top_chip))
            sibling = row + 1 - 2 * core
            for q in range(nx):
                part = wide.at[s, t, pl.ds(q * piece, piece)]

                @pl.when(full & (chip != q))
                def _():
                    landed(part, wide_sems.at[s, t, q])
                posted.send(full, part, part, wide_sems.at[s, t, q], sibling, col)
                posted.send(source & (side == 1), own.at[pl.ds(q * piece, piece)], part,
                            wide_sems.at[s, t, q], sibling, col)

    def leaf_wait(s, t):
        src = source_row(s, t)

        @pl.when((row < src) & (core != src % 2))
        def _():
            for q in range(nx):
                landed(wide.at[s, t, pl.ds(q * piece, piece)], wide_sems.at[s, t, q])

    def flip_wait(s, t):
        held = source_row(s, t) > row
        if s != 1:
            @pl.when(held)
            def _():
                landed(flip.at[s, t], flip_sems.at[s, t])

    @pl.when(role[0])
    def _():
        solve()
    spread(0)
    hand_on(False)
    relay(0)

    for t in range(2):
        for s in (0, 2):
            flip_wait(s, t)

    exists_row = row + 1 <= last
    @pl.when(role[1])
    def _():
        left = split(flip[0, slot])
        landed(a_far.at[0], far_sems.at[2])
        tmp_hi[...], tmp_lo[...] = transposed(a_far.at[0])
        landed(x_near.at[0], near_sems.at[0])
        acc[...] -= product(left, split(x_near[0]))
        landed(x_near.at[1], near_sems.at[1])
        acc[...] -= product(split(x_near[1]), (tmp_hi[...], tmp_lo[...]))
        solve()
    spread(1)
    relay(1)

    @pl.when(role[2])
    def _():
        landed(a_far.at[1], far_sems.at[3])
        tmp_hi[...], tmp_lo[...] = transposed(a_far.at[1])
        landed(x_near.at[2], near_sems.at[2])
        acc[...] -= product(split(flip[0, slot]), split(x_near[2]))
        landed(x_near.at[3], near_sems.at[3])
        acc[...] -= product(split(x_near[3]), (tmp_hi[...], tmp_lo[...]))
        landed(a_far.at[0], far_sems.at[2])
        tmp_hi[...], tmp_lo[...] = transposed(a_far.at[0])
        left = split(flip[1, slot])
        landed(x_near.at[0], near_sems.at[0])
        acc[...] -= product(left, split(x_near[0]))
        landed(x_near.at[1], near_sems.at[1])
        acc[...] -= product(split(x_near[1]), (tmp_hi[...], tmp_lo[...]))
        solve()
    spread(2)

    for s in range(FRONTS):
        if s == FRONTS - 1:
            relay(s)
        for t in range(2):
            leaf_wait(s, t)

            @pl.when(lags[t] >= FRONTS)
            def _():
                change = product(split(flip[s, t]), split(wide[s, t]))
                base = state[t] if s == 0 else out[t]
                out[t] = base - change
    for t in range(2):
        @pl.when(lags[t] < 0)
        def _():
            out[t] = state[t]

        @pl.when((lags[t] >= 0) & (lags[t] < FRONTS))
        def _():
            out[t] = own[...]
    posted.drain()


def per_device(nx, state, a_tiles, inverses):
    nc, nt = lax.axis_size("col"), lax.axis_size("row")
    order = inverses.shape[-1]
    tile = (order, order)
    in_vmem = pl.BlockSpec(memory_space=pltpu.VMEM)
    dma = pltpu.SemaphoreType.DMA
    result = pl.pallas_call(
        functools.partial(sweep, nt, nc, nx),
        out_shape=jax.ShapeDtypeStruct((2,) + tile, F32),
        in_specs=[in_vmem] * 3,
        out_specs=in_vmem,
        scratch_shapes=[
            pltpu.VMEM((FRONTS, 2) + tile, F32),
            pltpu.VMEM((FRONTS, 2) + tile, F32),
            pltpu.VMEM(tile, F32),
            pltpu.VMEM(tile, F32),
            pltpu.VMEM((2,) + tile, F32),
            pltpu.VMEM((4,) + tile, F32),
            pltpu.VMEM(tile, F32),
            pltpu.VMEM(tile, F32),
            pltpu.VMEM((DOUBLINGS,) + tile, BF16),
            pltpu.VMEM((DOUBLINGS,) + tile, BF16),
            pltpu.VMEM((DOUBLINGS,) + tile, BF16),
            pltpu.VMEM((DOUBLINGS,) + tile, BF16),
            pltpu.VMEM(tile, BF16),
            pltpu.VMEM(tile, BF16),
            dma((N_SENDS,)),
            dma((FRONTS, 2)),
            dma((FRONTS, 2, nx)),
            dma((4,)),
            dma((4,)),
        ],
        compiler_params=pltpu.CompilerParams(has_side_effects=True),
    )(state.reshape((2,) + tile), a_tiles.reshape((2,) + tile), inverses.reshape(tile))
    return result.reshape(state.shape)


def solution(mesh, nx=X_CHIPS):
    tiles = P("row", None, "col", None, None)
    return jax.shard_map(
        functools.partial(per_device, nx), mesh=mesh,
        in_specs=(tiles, tiles, P("row", None, None)), out_specs=tiles, check_vma=False,
    )
```

```python
import functools

import jax
import jax.numpy as jnp
from jax import lax
from jax.experimental import pallas as pl
from jax.experimental.pallas import tpu as pltpu
from jax.sharding import PartitionSpec as P

FRONTS = 3
DOUBLINGS = 5
X_CHIPS = 4
F32 = jnp.float32
BF16 = jnp.bfloat16
MESH = pl.DeviceIdType.MESH


def split(value):
    high = value.astype(BF16)
    low = (value - high.astype(F32)).astype(BF16)
    return high, low


def dot(left, right):
    return jnp.dot(left, right, preferred_element_type=F32)


def product(left, right):
    return dot(left[0], right[0]) + (dot(left[0], right[1]) + dot(left[1], right[0]))


class Posted:
    def __init__(self, sems):
        self.sems = sems
        self.items = []

    def send(self, condition, src, dst, recv_sem, row, col):
        copy = pltpu.make_async_remote_copy(
            src_ref=src, dst_ref=dst, send_sem=self.sems.at[len(self.items)],
            recv_sem=recv_sem, device_id=(row, col), device_id_type=MESH,
        )
        self.items.append((condition, copy))

        @pl.when(condition)
        def _():
            copy.start()

    def drain(self):
        for condition, copy in self.items:
            @pl.when(condition)
            def _():
                copy.wait_send()


def landed(ref, sem):
    pltpu.make_async_copy(ref, ref, sem).wait()


N_SENDS = 192


def sweep(nt, nc, nx, state, coupling, inverse, out,
          flip, wide, inv_far, h_far, a_far, x_near, own, acc,
          left_hi, left_lo, right_hi, right_lo, tmp_hi, tmp_lo,
          send_sems, flip_sems, wide_sems, far_sems, near_sems):
    order = inverse.shape[-1]
    piece = order // nx
    per_plane = 2 * nx
    planes = nt // per_plane
    row, col = lax.axis_index("row"), lax.axis_index("col")
    plane, chip, core = row // per_plane, (row // 2) % nx, row % 2
    posted = Posted(send_sems)
    last = nt - 1
    lag = last - col - row
    role = [(lag == s) | (lag == s + nc) for s in range(FRONTS)]
    slot = jnp.where(lag >= nc, 1, 0)
    lags = [lag, lag - nc]

    def source_row(s, t):
        return last - s - nc * t - col

    barrier = pltpu.get_barrier_semaphore()
    greeted = []

    def greet(condition, target_row, target_col):
        @pl.when(condition)
        def _():
            pl.semaphore_signal(barrier, inc=1, device_id=(target_row, target_col), device_id_type=MESH)

    def expect(condition):
        greeted.append(jnp.where(condition, 1, 0))

    for s in range(FRONTS):
        other = last - s - row
        apart = role[s] & (other != row)
        greet(apart, other, row % nc)
        expect(apart)
        greet(apart, other, col)
        expect((col == row % nc) & (other >= 0) & (other != row))
        for step in range(1, s + 1):
            greet(role[s], other, (other + step) % nc)
            expect((col == (row + step) % nc) & (other >= 0) & (row + step <= last))
            greet(role[s], row + step, col)
            greet(role[s], row, (col + step) % nc)
        for step in range(1, FRONTS - s):
            expect(role[s] & (row >= step))
            expect(role[s] & (other >= step))
    paired = (col != nc - 1) & (2 * col != nc - 2)
    greet(paired, row, nc - 2 - col)
    expect(paired)
    greet((col == 0) & (row < last), row, nc - 1)
    expect((col == nc - 1) & (row < last))
    every = row >= 0
    for step in (1, nc - 1):
        greet(every, row, (col + step) % nc)
        expect(every)
    for step in range(1, nx):
        greet(every, plane * per_plane + (row + 2 * step) % per_plane, col)
        expect(every)
    for step in range(1, planes):
        greet(every, (row + step * per_plane) % nt, col)
        expect(every)
    greet(every, row + 1 - 2 * core, col)
    expect(every)
    pl.semaphore_wait(barrier, functools.reduce(lambda x, y: x + y, greeted))

    for s in range(FRONTS):
        other = last - s - row
        posted.send(role[s] & (other != row), state.at[slot], h_far, far_sems.at[0], other, row % nc)
        posted.send((col == row % nc) & (other >= 0) & (other != row),
                    inverse, inv_far, far_sems.at[1], other, col)
        for step in range(1, s + 1):
            posted.send((col == (row + step) % nc) & (other >= 0) & (row + step <= last),
                        coupling.at[(row + step) // nc % 2], a_far.at[step - 1], far_sems.at[1 + step],
                        other, row % nc)

    for u in range(2):
        used = nc * u + col > row
        posted.send(used & (col != nc - 1) & (2 * col != nc - 2), coupling.at[u], flip.at[1, 1 - u],
                    flip_sems.at[1, 1 - u], row, nc - 2 - col)
    posted.send((col == nc - 1) & (last > row), coupling.at[1], flip.at[0, 0], flip_sems.at[0, 0], row, 0)
    for u in range(2):
        @pl.when((nc * u + col > row) & (2 * col == nc - 2))
        def _():
            flip[1, 1 - u] = coupling[u]

    @pl.when((nc - 1 > row) & (col == nc - 1))
    def _():
        flip[1, 0] = coupling[0]

    solver = role[0] | role[1] | role[2]
    flip_local = (2 * col == nc - 2) | (col == nc - 1)

    def hand_on(early):
        now = ~role[0] if early else role[0]
        for t in range(2):
            held = source_row(1, t) > row

            @pl.when(now & held & ~flip_local)
            def _():
                landed(flip.at[1, t], flip_sems.at[1, t])
            up = t + jnp.where(col == nc - 1, 1, 0)
            posted.send(now & held, flip.at[1, t], flip.at[0, up % 2], flip_sems.at[0, up % 2],
                        row, (col + 1) % nc)
            down = t - jnp.where(col == 0, 1, 0)
            posted.send(now & held & (down >= 0), flip.at[1, t], flip.at[2, down % 2],
                        flip_sems.at[2, down % 2], row, (col + nc - 1) % nc)

    hand_on(True)

    eye = (lax.broadcasted_iota(jnp.int32, (order, order), 0)
           == lax.broadcasted_iota(jnp.int32, (order, order), 1)).astype(F32)

    def powers(first, high, low):
        acc[...] = first

        def step(m, carry):
            value = split(acc[...])
            high[m], low[m] = value
            acc[...] = product(value, value)
            return carry
        lax.fori_loop(0, DOUBLINGS - 1, step, 0)
        high[DOUBLINGS - 1], low[DOUBLINGS - 1] = split(acc[...])

    self_mirror = role[1] & (2 * row == last - 1)
    mirrored = solver & ~self_mirror

    @pl.when(solver)
    def _():
        powers(eye - 0.5 * inverse[...], left_hi, left_lo)

        @pl.when(mirrored)
        def _():
            landed(inv_far, far_sems.at[1])

        @pl.when(self_mirror)
        def _():
            inv_far[...] = inverse[...]
            h_far[...] = state[slot]
        inv_far[...] = inv_far[...].T
        powers(eye - 0.5 * inv_far[...], right_hi, right_lo)

        @pl.when(mirrored)
        def _():
            landed(h_far, far_sems.at[0])
        acc[...] = state[slot] + h_far[...].T

    def transposed(ref):
        return split(ref[...].T)

    def solve():
        first = product(split(inverse[...]), split(acc[...]))
        own[...] = 0.5 * product(split(first), split(inv_far[...]))

        def level(m, carry):
            value = own[...]
            middle = product((left_hi[m], left_lo[m]), split(value))
            own[...] = value + product(split(middle), (right_hi[m], right_lo[m]))
            return carry
        lax.fori_loop(0, DOUBLINGS, level, 0)

    def spread(s):
        mirror = last - s - row
        for step in range(1, FRONTS - s):
            spot = 2 * (step - 1)
            if s + step == 2 and step == 1:
                spot = 0
            posted.send(role[s] & (row >= step), own, x_near.at[spot], near_sems.at[spot], row - step, col)
            posted.send(role[s] & (mirror >= step), own, x_near.at[spot + 1], near_sems.at[spot + 1],
                        row, (col + nc - step) % nc)
        for q in range(nx):
            posted.send(role[s] & (row >= 1) & (chip != q), own.at[pl.ds(q * piece, piece)],
                        wide.at[s, slot, pl.ds(q * piece, piece)], wide_sems.at[s, slot, q],
                        plane * per_plane + 2 * q + core, col)

    def relay(s):
        for t in range(2):
            src = source_row(s, t)
            top_plane, top_chip, side = src // per_plane, (src // 2) % nx, src % 2
            live = src >= 1
            here = live & (core == side)
            source = here & (row == src)
            level = here & (plane == top_plane)
            below = here & (plane < top_plane)
            span = pl.ds(pl.multiple_of(chip * piece, 8), piece)
            mine = wide.at[s, t, span]
            own_part = own.at[span]

            @pl.when((level & ~source) | below)
            def _():
                landed(mine, wide_sems.at[s, t, chip])
            for target in range(planes - 1):
                go = level & (target < top_plane)
                dst_row = target * per_plane + 2 * chip + core
                posted.send(go & ~source, mine, mine, wide_sems.at[s, t, chip], dst_row, col)
                posted.send(go & source, own_part, mine, wide_sems.at[s, t, chip], dst_row, col)
            for q in range(nx):
                go = (chip != q) & (below | (level & (q < top_chip)))
                dst_row = plane * per_plane + 2 * q + core
                posted.send(go & ~source, mine, mine, wide_sems.at[s, t, chip], dst_row, col)
                posted.send(go & source, own_part, mine, wide_sems.at[s, t, chip], dst_row, col)
            full = below | (level & (chip < top_chip))
            sibling = row + 1 - 2 * core
            for q in range(nx):
                part = wide.at[s, t, pl.ds(q * piece, piece)]

                @pl.when(full & (chip != q))
                def _():
                    landed(part, wide_sems.at[s, t, q])
                posted.send(full, part, part, wide_sems.at[s, t, q], sibling, col)
                posted.send(source & (side == 1), own.at[pl.ds(q * piece, piece)], part,
                            wide_sems.at[s, t, q], sibling, col)

    def leaf_wait(s, t):
        src = source_row(s, t)

        @pl.when((row < src) & (core != src % 2))
        def _():
            for q in range(nx):
                landed(wide.at[s, t, pl.ds(q * piece, piece)], wide_sems.at[s, t, q])

    def flip_wait(s, t):
        held = source_row(s, t) > row
        if s != 1:
            @pl.when(held)
            def _():
                landed(flip.at[s, t], flip_sems.at[s, t])

    @pl.when(role[0])
    def _():
        solve()
    spread(0)
    hand_on(False)
    relay(0)

    for t in range(2):
        for s in (0, 2):
            flip_wait(s, t)

    exists_row = row + 1 <= last
    @pl.when(role[1])
    def _():
        left = split(flip[0, slot])
        landed(a_far.at[0], far_sems.at[2])
        tmp_hi[...], tmp_lo[...] = transposed(a_far.at[0])
        landed(x_near.at[0], near_sems.at[0])
        acc[...] -= product(left, split(x_near[0]))
        landed(x_near.at[1], near_sems.at[1])
        acc[...] -= product(split(x_near[1]), (tmp_hi[...], tmp_lo[...]))
        solve()
    spread(1)
    relay(1)

    @pl.when(role[2])
    def _():
        landed(a_far.at[1], far_sems.at[3])
        tmp_hi[...], tmp_lo[...] = transposed(a_far.at[1])
        landed(x_near.at[2], near_sems.at[2])
        acc[...] -= product(split(flip[0, slot]), split(x_near[2]))
        landed(x_near.at[3], near_sems.at[3])
        acc[...] -= product(split(x_near[3]), (tmp_hi[...], tmp_lo[...]))
        landed(a_far.at[0], far_sems.at[2])
        tmp_hi[...], tmp_lo[...] = transposed(a_far.at[0])
        left = split(flip[1, slot])
        landed(x_near.at[0], near_sems.at[0])
        acc[...] -= product(left, split(x_near[0]))
        landed(x_near.at[1], near_sems.at[1])
        acc[...] -= product(split(x_near[1]), (tmp_hi[...], tmp_lo[...]))
        solve()
    spread(2)

    for s in range(FRONTS):
        if s == FRONTS - 1:
            relay(s)
        for t in range(2):
            leaf_wait(s, t)

            @pl.when(lags[t] >= FRONTS)
            def _():
                change = product(split(flip[s, t]), split(wide[s, t]))
                base = state[t] if s == 0 else out[t]
                out[t] = base - change
    for t in range(2):
        @pl.when(lags[t] < 0)
        def _():
            out[t] = state[t]

        @pl.when((lags[t] >= 0) & (lags[t] < FRONTS))
        def _():
            out[t] = own[...]
    posted.drain()


def per_device(nx, state, a_tiles, inverses):
    nc, nt = lax.axis_size("col"), lax.axis_size("row")
    order = inverses.shape[-1]
    tile = (order, order)
    in_vmem = pl.BlockSpec(memory_space=pltpu.VMEM)
    dma = pltpu.SemaphoreType.DMA
    result = pl.pallas_call(
        functools.partial(sweep, nt, nc, nx),
        out_shape=jax.ShapeDtypeStruct((2,) + tile, F32),
        in_specs=[in_vmem] * 3,
        out_specs=in_vmem,
        scratch_shapes=[
            pltpu.VMEM((FRONTS, 2) + tile, F32),
            pltpu.VMEM((FRONTS, 2) + tile, F32),
            pltpu.VMEM(tile, F32),
            pltpu.VMEM(tile, F32),
            pltpu.VMEM((2,) + tile, F32),
            pltpu.VMEM((4,) + tile, F32),
            pltpu.VMEM(tile, F32),
            pltpu.VMEM(tile, F32),
            pltpu.VMEM((DOUBLINGS,) + tile, BF16),
            pltpu.VMEM((DOUBLINGS,) + tile, BF16),
            pltpu.VMEM((DOUBLINGS,) + tile, BF16),
            pltpu.VMEM((DOUBLINGS,) + tile, BF16),
            pltpu.VMEM(tile, BF16),
            pltpu.VMEM(tile, BF16),
            dma((N_SENDS,)),
            dma((FRONTS, 2)),
            dma((FRONTS, 2, nx)),
            dma((4,)),
            dma((4,)),
        ],
        compiler_params=pltpu.CompilerParams(collective_id=0, has_side_effects=True),
    )(state.reshape((2,) + tile), a_tiles.reshape((2,) + tile), inverses.reshape(tile))
    return result.reshape(state.shape)


def solution(mesh, nx=X_CHIPS):
    tiles = P("row", None, "col", None, None)
    return jax.shard_map(
        functools.partial(per_device, nx), mesh=mesh,
        in_specs=(tiles, tiles, P("row", None, None)), out_specs=tiles, check_vma=False,
    )
```

```python
import functools

import jax
import jax.numpy as jnp
from jax import lax
from jax.experimental import pallas as pl
from jax.experimental.pallas import tpu as pltpu
from jax.sharding import PartitionSpec as P

FRONTS = 3
DOUBLINGS = 5
X_CHIPS = 4
F32 = jnp.float32
BF16 = jnp.bfloat16
MESH = pl.DeviceIdType.MESH


def split(value):
    high = value.astype(BF16)
    low = (value - high.astype(F32)).astype(BF16)
    return high, low


def dot(left, right):
    return jnp.dot(left, right, preferred_element_type=F32)


def product(left, right):
    return dot(left[0], right[0]) + (dot(left[0], right[1]) + dot(left[1], right[0]))


class Posted:
    def __init__(self, sems):
        self.sems = sems
        self.items = []

    def send(self, condition, src, dst, recv_sem, row, col):
        copy = pltpu.make_async_remote_copy(
            src_ref=src, dst_ref=dst, send_sem=self.sems.at[len(self.items)],
            recv_sem=recv_sem, device_id=(row, col), device_id_type=MESH,
        )
        self.items.append((condition, copy))

        @pl.when(condition)
        def _():
            copy.start()

    def drain(self):
        for condition, copy in self.items:
            @pl.when(condition)
            def _():
                copy.wait_send()


def landed(ref, sem):
    pltpu.make_async_copy(ref, ref, sem).wait()


N_SENDS = 192


def sweep(nt, nc, nx, state, coupling, inverse, out,
          flip, wide, inv_far, h_far, a_far, a_near, x_near, own, acc,
          left_hi, left_lo, right_hi, right_lo, tmp_hi, tmp_lo,
          send_sems, flip_sems, wide_sems, far_sems, near_sems, go):
    order = inverse.shape[-1]
    piece = order // nx
    per_plane = 2 * nx
    planes = nt // per_plane
    row, col = lax.axis_index("row"), lax.axis_index("col")
    plane, chip, core = row // per_plane, (row // 2) % nx, row % 2
    posted = Posted(send_sems)
    last = nt - 1
    lag = last - col - row
    role = [(lag == s) | (lag == s + nc) for s in range(FRONTS)]
    slot = jnp.where(lag >= nc, 1, 0)
    lags = [lag, lag - nc]

    def source_row(s, t):
        return last - s - nc * t - col

    barrier = pltpu.get_barrier_semaphore()
    greeted = []

    def greet(condition, target_row, target_col):
        @pl.when(condition)
        def _():
            pl.semaphore_signal(barrier, inc=1, device_id=(target_row, target_col), device_id_type=MESH)

    def expect(condition):
        greeted.append(jnp.where(condition, 1, 0))

    for s in range(FRONTS):
        other = last - s - row
        apart = role[s] & (other != row)
        greet(apart, other, row % nc)
        expect(apart)
        greet(apart, other, col)
        expect((col == row % nc) & (other >= 0) & (other != row))
        for step in range(1, s + 1):
            greet(role[s], other, (other + step) % nc)
            expect((col == (row + step) % nc) & (other >= 0) & (row + step <= last))
            near = (col == (row + step) % nc) & (other >= 0) & (row + step <= last)
            apart = (row + step) % nc != other % nc
            greet(role[s] & apart, row, (row + step) % nc)
            expect(near & apart)
            greet(role[s], row + step, col)
            greet(role[s], row, (col + step) % nc)
        for step in range(1, FRONTS - s):
            expect(role[s] & (row >= step))
            expect(role[s] & (other >= step))
    paired = (col != nc - 1) & (2 * col != nc - 2)
    greet(paired, row, nc - 2 - col)
    expect(paired)
    greet((col == 0) & (row < last), row, nc - 1)
    expect((col == nc - 1) & (row < last))
    every = row >= 0
    first_col = (last - row) % nc
    greet(col != first_col, row, first_col)
    greeted.append(jnp.where(role[0], nc - 1, 0))
    for step in (1, nc - 1):
        greet(every, row, (col + step) % nc)
        expect(every)
    for step in range(1, nx):
        greet(every, plane * per_plane + (row + 2 * step) % per_plane, col)
        expect(every)
    for step in range(1, planes):
        greet(every, (row + step * per_plane) % nt, col)
        expect(every)
    greet(every, row + 1 - 2 * core, col)
    expect(every)
    pl.semaphore_wait(barrier, functools.reduce(lambda x, y: x + y, greeted))

    for s in range(FRONTS):
        other = last - s - row
        posted.send(role[s] & (other != row), state.at[slot], h_far, far_sems.at[0], other, row % nc)
        posted.send((col == row % nc) & (other >= 0) & (other != row),
                    inverse, inv_far, far_sems.at[1], other, col)
        for step in range(1, s + 1):
            posted.send((col == (row + step) % nc) & (other >= 0) & (row + step <= last),
                        coupling.at[(row + step) // nc % 2], a_far.at[step - 1], far_sems.at[1 + step],
                        other, row % nc)
            apart = (row + step) % nc != other % nc
            holder = (col == (row + step) % nc) & (other >= 0) & (row + step <= last)
            posted.send(holder & apart, coupling.at[(row + step) // nc % 2], a_near.at[step - 1],
                        far_sems.at[3 + step], row, other % nc)

            @pl.when(holder & ~apart)
            def _():
                a_near[step - 1] = coupling[(row + step) // nc % 2]

    solver = role[0] | role[1] | role[2]

    flip_local = (2 * col == nc - 2) | (col == nc - 1)

    def reflect(now):
        for u in range(2):
            used = nc * u + col > row
            posted.send(now & used & ~flip_local, coupling.at[u], flip.at[1, 1 - u],
                        flip_sems.at[1, 1 - u], row, nc - 2 - col)
            beside = (2 * col == nc - 4) if u == 1 else (2 * col == nc - 4) | (col == nc - 2)
            to = jnp.where(col == nc - 2, 0, 1) if u == 0 else 0
            posted.send(now & used & beside, coupling.at[u], flip.at[2, to], flip_sems.at[2, to], row, (col + 1) % nc)
        posted.send(now & (col == nc - 1) & (last > row), coupling.at[1], flip.at[0, 0], flip_sems.at[0, 0], row, 0)

    for u in range(2):
        @pl.when((nc * u + col > row) & (2 * col == nc - 2))
        def _():
            flip[1, 1 - u] = coupling[u]

    @pl.when((nc - 1 > row) & (col == nc - 1))
    def _():
        flip[1, 0] = coupling[0]

    def hand_on(now):
        for t in range(2):
            held = source_row(1, t) > row

            @pl.when(now & held & ~flip_local)
            def _():
                landed(flip.at[1, t], flip_sems.at[1, t])
            up = t + jnp.where(col == nc - 1, 1, 0)
            posted.send(now & held, flip.at[1, t], flip.at[0, up % 2], flip_sems.at[0, up % 2],
                        row, (col + 1) % nc)
            posted.send(now & held & (col != 0) & (2 * col != nc), flip.at[1, t], flip.at[2, t],
                        flip_sems.at[2, t], row, (col + nc - 1) % nc)

    eye = (lax.broadcasted_iota(jnp.int32, (order, order), 0)
           == lax.broadcasted_iota(jnp.int32, (order, order), 1)).astype(F32)

    def powers(first, high, low):
        acc[...] = first

        def step(m, carry):
            value = split(acc[...])
            high[m], low[m] = value
            acc[...] = product(value, value)
            return carry
        lax.fori_loop(0, DOUBLINGS - 1, step, 0)
        high[DOUBLINGS - 1], low[DOUBLINGS - 1] = split(acc[...])

    self_mirror = role[1] & (2 * row == last - 1)
    mirrored = solver & ~self_mirror

    @pl.when(solver)
    def _():
        powers(eye - 0.5 * inverse[...], left_hi, left_lo)

        @pl.when(mirrored)
        def _():
            landed(inv_far, far_sems.at[1])

        @pl.when(self_mirror)
        def _():
            inv_far[...] = inverse[...]
            h_far[...] = state[slot]
        inv_far[...] = inv_far[...].T
        powers(eye - 0.5 * inv_far[...], right_hi, right_lo)

        @pl.when(mirrored)
        def _():
            landed(h_far, far_sems.at[0])
        acc[...] = state[slot] + h_far[...].T

    for step in range(1, nc):
        @pl.when(role[0])
        def _():
            pl.semaphore_signal(go, inc=1, device_id=(row, (col + step) % nc), device_id_type=MESH)

    @pl.when(~role[0])
    def _():
        pl.semaphore_wait(go, 1)
    reflect(~role[0])
    hand_on(~solver)

    def transposed(ref):
        return split(ref[...].T)

    def solve():
        first = product(split(inverse[...]), split(acc[...]))
        own[...] = 0.5 * product(split(first), split(inv_far[...]))

        def level(m, carry):
            value = own[...]
            middle = product((left_hi[m], left_lo[m]), split(value))
            own[...] = value + product(split(middle), (right_hi[m], right_lo[m]))
            return carry
        lax.fori_loop(0, DOUBLINGS, level, 0)

    def spread(s):
        mirror = last - s - row
        for step in range(1, FRONTS - s):
            spot = 2 * (step - 1)
            if s + step == 2 and step == 1:
                spot = 0
            posted.send(role[s] & (row >= step), own, x_near.at[spot], near_sems.at[spot], row - step, col)
            posted.send(role[s] & (mirror >= step), own, x_near.at[spot + 1], near_sems.at[spot + 1],
                        row, (col + nc - step) % nc)
        for q in range(nx):
            posted.send(role[s] & (row >= 1) & (chip != q), own.at[pl.ds(q * piece, piece)],
                        wide.at[s, slot, pl.ds(q * piece, piece)], wide_sems.at[s, slot, q],
                        plane * per_plane + 2 * q + core, col)

    def relay(s):
        for t in range(2):
            src = source_row(s, t)
            top_plane, top_chip, side = src // per_plane, (src // 2) % nx, src % 2
            live = src >= 1
            here = live & (core == side)
            source = here & (row == src)
            level = here & (plane == top_plane)
            below = here & (plane < top_plane)
            span = pl.ds(pl.multiple_of(chip * piece, 8), piece)
            mine = wide.at[s, t, span]
            own_part = own.at[span]

            @pl.when((level & ~source) | below)
            def _():
                landed(mine, wide_sems.at[s, t, chip])
            for target in range(planes - 1):
                go = level & (target < top_plane)
                dst_row = target * per_plane + 2 * chip + core
                posted.send(go & ~source, mine, mine, wide_sems.at[s, t, chip], dst_row, col)
                posted.send(go & source, own_part, mine, wide_sems.at[s, t, chip], dst_row, col)
            for q in range(nx):
                go = (chip != q) & (below | (level & (q < top_chip)))
                dst_row = plane * per_plane + 2 * q + core
                posted.send(go & ~source, mine, mine, wide_sems.at[s, t, chip], dst_row, col)
                posted.send(go & source, own_part, mine, wide_sems.at[s, t, chip], dst_row, col)
            full = below | (level & (chip < top_chip))
            sibling = row + 1 - 2 * core
            for q in range(nx):
                part = wide.at[s, t, pl.ds(q * piece, piece)]

                @pl.when(full & (chip != q))
                def _():
                    landed(part, wide_sems.at[s, t, q])
                posted.send(full, part, part, wide_sems.at[s, t, q], sibling, col)
                posted.send(source & (side == 1), own.at[pl.ds(q * piece, piece)], part,
                            wide_sems.at[s, t, q], sibling, col)

    def leaf_wait(s, t):
        src = source_row(s, t)

        @pl.when((row < src) & (core != src % 2))
        def _():
            for q in range(nx):
                landed(wide.at[s, t, pl.ds(q * piece, piece)], wide_sems.at[s, t, q])

    def flip_wait(s, t):
        held = source_row(s, t) > row
        if s != 1:
            @pl.when(held)
            def _():
                landed(flip.at[s, t], flip_sems.at[s, t])

    @pl.when(role[0])
    def _():
        solve()
    spread(0)
    reflect(role[0])
    hand_on(role[0])
    relay(0)

    @pl.when(role[1])
    def _():
        landed(a_near.at[0], far_sems.at[4])
        left = split(a_near[0])
        landed(a_far.at[0], far_sems.at[2])
        tmp_hi[...], tmp_lo[...] = transposed(a_far.at[0])
        landed(x_near.at[0], near_sems.at[0])
        acc[...] -= product(left, split(x_near[0]))
        landed(x_near.at[1], near_sems.at[1])
        acc[...] -= product(split(x_near[1]), (tmp_hi[...], tmp_lo[...]))
        solve()
    spread(1)
    hand_on(role[1])
    relay(1)

    @pl.when(role[2])
    def _():
        landed(a_far.at[1], far_sems.at[3])
        tmp_hi[...], tmp_lo[...] = transposed(a_far.at[1])
        landed(x_near.at[2], near_sems.at[2])
        landed(a_near.at[1], far_sems.at[5])
        acc[...] -= product(split(a_near[1]), split(x_near[2]))
        landed(x_near.at[3], near_sems.at[3])
        acc[...] -= product(split(x_near[3]), (tmp_hi[...], tmp_lo[...]))
        landed(a_far.at[0], far_sems.at[2])
        tmp_hi[...], tmp_lo[...] = transposed(a_far.at[0])

        @pl.when((row + 1) % nc != col)
        def _():
            landed(a_near.at[0], far_sems.at[4])
        left = split(a_near[0])
        landed(x_near.at[0], near_sems.at[0])
        acc[...] -= product(left, split(x_near[0]))
        landed(x_near.at[1], near_sems.at[1])
        acc[...] -= product(split(x_near[1]), (tmp_hi[...], tmp_lo[...]))
        solve()
    spread(2)
    hand_on(role[2])

    for s in range(FRONTS):
        if s == FRONTS - 1:
            relay(s)
        for t in range(2):
            if s != 1:
                flip_wait(s, t)
            leaf_wait(s, t)

            @pl.when(lags[t] >= FRONTS)
            def _():
                change = product(split(flip[s, t]), split(wide[s, t]))
                base = state[t] if s == 0 else out[t]
                out[t] = base - change
    for t in range(2):
        @pl.when(lags[t] < 0)
        def _():
            out[t] = state[t]

        @pl.when((lags[t] >= 0) & (lags[t] < FRONTS))
        def _():
            out[t] = own[...]
    posted.drain()


def per_device(nx, state, a_tiles, inverses):
    nc, nt = lax.axis_size("col"), lax.axis_size("row")
    order = inverses.shape[-1]
    tile = (order, order)
    in_vmem = pl.BlockSpec(memory_space=pltpu.VMEM)
    dma = pltpu.SemaphoreType.DMA
    result = pl.pallas_call(
        functools.partial(sweep, nt, nc, nx),
        out_shape=jax.ShapeDtypeStruct((2,) + tile, F32),
        in_specs=[in_vmem] * 3,
        out_specs=in_vmem,
        scratch_shapes=[
            pltpu.VMEM((FRONTS, 2) + tile, F32),
            pltpu.VMEM((FRONTS, 2) + tile, F32),
            pltpu.VMEM(tile, F32),
            pltpu.VMEM(tile, F32),
            pltpu.VMEM((2,) + tile, F32),
            pltpu.VMEM((2,) + tile, F32),
            pltpu.VMEM((4,) + tile, F32),
            pltpu.VMEM(tile, F32),
            pltpu.VMEM(tile, F32),
            pltpu.VMEM((DOUBLINGS,) + tile, BF16),
            pltpu.VMEM((DOUBLINGS,) + tile, BF16),
            pltpu.VMEM((DOUBLINGS,) + tile, BF16),
            pltpu.VMEM((DOUBLINGS,) + tile, BF16),
            pltpu.VMEM(tile, BF16),
            pltpu.VMEM(tile, BF16),
            dma((N_SENDS,)),
            dma((FRONTS, 2)),
            dma((FRONTS, 2, nx)),
            dma((6,)),
            dma((4,)),
            pltpu.SemaphoreType.REGULAR,
        ],
        compiler_params=pltpu.CompilerParams(collective_id=0, has_side_effects=True),
    )(state.reshape((2,) + tile), a_tiles.reshape((2,) + tile), inverses.reshape(tile))
    return result.reshape(state.shape)


def solution(mesh, nx=X_CHIPS):
    tiles = P("row", None, "col", None, None)
    return jax.shard_map(
        functools.partial(per_device, nx), mesh=mesh,
        in_specs=(tiles, tiles, P("row", None, None)), out_specs=tiles, check_vma=False,
    )
```

```python
import functools

import jax
import jax.numpy as jnp
from jax import lax
from jax.experimental import pallas as pl
from jax.experimental.pallas import tpu as pltpu
from jax.sharding import PartitionSpec as P

FRONTS = 3
DOUBLINGS = 5
X_CHIPS = 4
F32 = jnp.float32
BF16 = jnp.bfloat16
MESH = pl.DeviceIdType.MESH


def split(value):
    high = value.astype(BF16)
    low = (value - high.astype(F32)).astype(BF16)
    return high, low


def dot(left, right):
    return jnp.dot(left, right, preferred_element_type=F32)


def product(left, right):
    return dot(left[0], right[0]) + (dot(left[0], right[1]) + dot(left[1], right[0]))


class Posted:
    def __init__(self, sems):
        self.sems = sems
        self.items = []

    def send(self, condition, src, dst, recv_sem, row, col):
        copy = pltpu.make_async_remote_copy(
            src_ref=src, dst_ref=dst, send_sem=self.sems.at[len(self.items)],
            recv_sem=recv_sem, device_id=(row, col), device_id_type=MESH,
        )
        self.items.append((condition, copy))

        @pl.when(condition)
        def _():
            copy.start()

    def drain(self):
        for condition, copy in self.items:
            @pl.when(condition)
            def _():
                copy.wait_send()


def landed(ref, sem):
    pltpu.make_async_copy(ref, ref, sem).wait()


N_SENDS = 192


def sweep(nt, nc, nx, state, coupling, inverse, out,
          flip, wide, inv_far, h_far, a_far, a_near, x_near, own, acc,
          left_hi, left_lo, right_hi, right_lo, tmp_hi, tmp_lo,
          send_sems, flip_sems, wide_sems, far_sems, near_sems, go):
    order = inverse.shape[-1]
    piece = order // nx
    per_plane = 2 * nx
    planes = nt // per_plane
    row, col = lax.axis_index("row"), lax.axis_index("col")
    plane, chip, core = row // per_plane, (row // 2) % nx, row % 2
    posted = Posted(send_sems)
    last = nt - 1
    lag = last - col - row
    role = [(lag == s) | (lag == s + nc) for s in range(FRONTS)]
    slot = jnp.where(lag >= nc, 1, 0)
    lags = [lag, lag - nc]

    def source_row(s, t):
        return last - s - nc * t - col

    barrier = pltpu.get_barrier_semaphore()
    greeted = []

    def greet(condition, target_row, target_col):
        @pl.when(condition)
        def _():
            pl.semaphore_signal(barrier, inc=1, device_id=(target_row, target_col), device_id_type=MESH)

    def expect(condition):
        greeted.append(jnp.where(condition, 1, 0))

    for s in range(FRONTS):
        other = last - s - row
        apart = role[s] & (other != row)
        greet(apart, other, row % nc)
        expect(apart)
        greet(apart, other, col)
        expect((col == row % nc) & (other >= 0) & (other != row))
        for step in range(1, s + 1):
            greet(role[s], other, (other + step) % nc)
            expect((col == (row + step) % nc) & (other >= 0) & (row + step <= last))
            if s == 1:
                greet(role[s], row, (row + step) % nc)
                expect((col == (row + step) % nc) & (other >= 0) & (row + step <= last))
            greet(role[s], row + step, col)
            greet(role[s], row, (col + step) % nc)
        for step in range(1, FRONTS - s):
            expect(role[s] & (row >= step))
            expect(role[s] & (other >= step))
    paired = (col != nc - 1) & (2 * col != nc - 2)
    greet(paired, row, nc - 2 - col)
    expect(paired)
    greet((col == 0) & (row < last), row, nc - 1)
    expect((col == nc - 1) & (row < last))
    every = row >= 0
    first_col = (last - row) % nc
    greet(col != first_col, row, first_col)
    greeted.append(jnp.where(role[0], nc - 1, 0))
    for step in (1, nc - 1):
        greet(every, row, (col + step) % nc)
        expect(every)
    for step in range(1, nx):
        greet(every, plane * per_plane + (row + 2 * step) % per_plane, col)
        expect(every)
    for step in range(1, planes):
        greet(every, (row + step * per_plane) % nt, col)
        expect(every)
    greet(every, row + 1 - 2 * core, col)
    expect(every)
    pl.semaphore_wait(barrier, functools.reduce(lambda x, y: x + y, greeted))

    def fetch(s, now):
        other = last - s - row
        posted.send(now & role[s] & (other != row), state.at[slot], h_far, far_sems.at[0], other, row % nc)
        posted.send(now & (col == row % nc) & (other >= 0) & (other != row),
                    inverse, inv_far, far_sems.at[1], other, col)
        for step in range(1, s + 1):
            holder = now & (col == (row + step) % nc) & (other >= 0) & (row + step <= last)
            tile = coupling.at[(row + step) // nc % 2]
            if s == 1:
                posted.send(holder, tile, a_near, far_sems.at[4], row, other % nc)
            posted.send(holder, tile, a_far.at[step - 1], far_sems.at[1 + step], other, row % nc)

    fetch(0, every)
    fetch(1, every)
    solver = role[0] | role[1] | role[2]

    flip_local = (2 * col == nc - 2) | (col == nc - 1)

    def reflect(now):
        for u in range(2):
            used = nc * u + col > row
            posted.send(now & used & ~flip_local, coupling.at[u], flip.at[1, 1 - u],
                        flip_sems.at[1, 1 - u], row, nc - 2 - col)
            beside = (2 * col == nc - 4) if u == 1 else (2 * col == nc - 4) | (col == nc - 2)
            to = jnp.where(col == nc - 2, 0, 1) if u == 0 else 0
            posted.send(now & used & beside, coupling.at[u], flip.at[2, to], flip_sems.at[2, to], row, (col + 1) % nc)
        posted.send(now & (col == nc - 1) & (last > row), coupling.at[1], flip.at[0, 0], flip_sems.at[0, 0], row, 0)

    for u in range(2):
        @pl.when((nc * u + col > row) & (2 * col == nc - 2))
        def _():
            flip[1, 1 - u] = coupling[u]

    @pl.when((nc - 1 > row) & (col == nc - 1))
    def _():
        flip[1, 0] = coupling[0]

    def hand_on(now):
        for t in range(2):
            held = source_row(1, t) > row

            @pl.when(now & held & ~flip_local)
            def _():
                landed(flip.at[1, t], flip_sems.at[1, t])
            up = t + jnp.where(col == nc - 1, 1, 0)
            posted.send(now & held, flip.at[1, t], flip.at[0, up % 2], flip_sems.at[0, up % 2],
                        row, (col + 1) % nc)
            posted.send(now & held & (col != 0) & (2 * col != nc), flip.at[1, t], flip.at[2, t],
                        flip_sems.at[2, t], row, (col + nc - 1) % nc)

    eye = (lax.broadcasted_iota(jnp.int32, (order, order), 0)
           == lax.broadcasted_iota(jnp.int32, (order, order), 1)).astype(F32)

    def powers(first, high, low):
        acc[...] = first

        def step(m, carry):
            value = split(acc[...])
            high[m], low[m] = value
            acc[...] = product(value, value)
            return carry
        lax.fori_loop(0, DOUBLINGS - 1, step, 0)
        high[DOUBLINGS - 1], low[DOUBLINGS - 1] = split(acc[...])

    self_mirror = role[1] & (2 * row == last - 1)
    mirrored = solver & ~self_mirror

    def prepare():
        powers(eye - 0.5 * inverse[...], left_hi, left_lo)

        @pl.when(mirrored)
        def _():
            landed(inv_far, far_sems.at[1])

        @pl.when(self_mirror)
        def _():
            inv_far[...] = inverse[...]
            h_far[...] = state[slot]
        inv_far[...] = inv_far[...].T
        powers(eye - 0.5 * inv_far[...], right_hi, right_lo)

        @pl.when(mirrored)
        def _():
            landed(h_far, far_sems.at[0])
        acc[...] = state[slot] + h_far[...].T

    @pl.when(role[0])
    def _():
        prepare()

    for step in range(1, nc):
        @pl.when(role[0])
        def _():
            pl.semaphore_signal(go, inc=1, device_id=(row, (col + step) % nc), device_id_type=MESH)

    @pl.when(~role[0])
    def _():
        pl.semaphore_wait(go, 1)
    fetch(2, ~role[0])
    reflect(~role[0])
    hand_on(~solver)

    @pl.when(role[1] | role[2])
    def _():
        prepare()

    def transposed(ref):
        return split(ref[...].T)

    def solve():
        first = product(split(inverse[...]), split(acc[...]))
        own[...] = 0.5 * product(split(first), split(inv_far[...]))

        def level(m, carry):
            value = own[...]
            middle = product((left_hi[m], left_lo[m]), split(value))
            own[...] = value + product(split(middle), (right_hi[m], right_lo[m]))
            return carry
        lax.fori_loop(0, DOUBLINGS, level, 0)

    def spread(s):
        mirror = last - s - row
        for step in range(1, FRONTS - s):
            spot = 2 * (step - 1)
            if s + step == 2 and step == 1:
                spot = 0
            posted.send(role[s] & (row >= step), own, x_near.at[spot], near_sems.at[spot], row - step, col)
            posted.send(role[s] & (mirror >= step), own, x_near.at[spot + 1], near_sems.at[spot + 1],
                        row, (col + nc - step) % nc)
        for q in range(nx):
            posted.send(role[s] & (row >= 1) & (chip != q), own.at[pl.ds(q * piece, piece)],
                        wide.at[s, slot, pl.ds(q * piece, piece)], wide_sems.at[s, slot, q],
                        plane * per_plane + 2 * q + core, col)

    def relay(s):
        for t in range(2):
            src = source_row(s, t)
            top_plane, top_chip, side = src // per_plane, (src // 2) % nx, src % 2
            live = src >= 1
            here = live & (core == side)
            source = here & (row == src)
            level = here & (plane == top_plane)
            below = here & (plane < top_plane)
            span = pl.ds(pl.multiple_of(chip * piece, 8), piece)
            mine = wide.at[s, t, span]
            own_part = own.at[span]

            @pl.when((level & ~source) | below)
            def _():
                landed(mine, wide_sems.at[s, t, chip])
            for target in range(planes - 1):
                go = level & (target < top_plane)
                dst_row = target * per_plane + 2 * chip + core
                posted.send(go & ~source, mine, mine, wide_sems.at[s, t, chip], dst_row, col)
                posted.send(go & source, own_part, mine, wide_sems.at[s, t, chip], dst_row, col)
            for q in range(nx):
                go = (chip != q) & (below | (level & (q < top_chip)))
                dst_row = plane * per_plane + 2 * q + core
                posted.send(go & ~source, mine, mine, wide_sems.at[s, t, chip], dst_row, col)
                posted.send(go & source, own_part, mine, wide_sems.at[s, t, chip], dst_row, col)
            full = below | (level & (chip < top_chip))
            sibling = row + 1 - 2 * core
            for q in range(nx):
                part = wide.at[s, t, pl.ds(q * piece, piece)]

                @pl.when(full & (chip != q))
                def _():
                    landed(part, wide_sems.at[s, t, q])
                posted.send(full, part, part, wide_sems.at[s, t, q], sibling, col)
                posted.send(source & (side == 1), own.at[pl.ds(q * piece, piece)], part,
                            wide_sems.at[s, t, q], sibling, col)

    def leaf_wait(s, t):
        src = source_row(s, t)

        @pl.when((row < src) & (core != src % 2))
        def _():
            for q in range(nx):
                landed(wide.at[s, t, pl.ds(q * piece, piece)], wide_sems.at[s, t, q])

    def flip_wait(s, t, now):
        held = source_row(s, t) > row

        @pl.when(now & held)
        def _():
            landed(flip.at[s, t], flip_sems.at[s, t])

    @pl.when(role[0])
    def _():
        solve()
    spread(0)
    fetch(2, role[0])
    reflect(role[0])
    hand_on(role[0])
    relay(0)

    @pl.when(role[1])
    def _():
        landed(a_near, far_sems.at[4])
        left = split(a_near[...])
        landed(a_far.at[0], far_sems.at[2])
        tmp_hi[...], tmp_lo[...] = transposed(a_far.at[0])
        landed(x_near.at[0], near_sems.at[0])
        acc[...] -= product(left, split(x_near[0]))
        landed(x_near.at[1], near_sems.at[1])
        acc[...] -= product(split(x_near[1]), (tmp_hi[...], tmp_lo[...]))
        solve()
    spread(1)
    hand_on(role[1])
    relay(1)
    hand_on(role[2])
    for t in range(2):
        flip_wait(0, t, role[2])

    @pl.when(role[2])
    def _():
        landed(a_far.at[1], far_sems.at[3])
        tmp_hi[...], tmp_lo[...] = transposed(a_far.at[1])
        landed(x_near.at[2], near_sems.at[2])
        acc[...] -= product(split(flip[0, slot]), split(x_near[2]))
        landed(x_near.at[3], near_sems.at[3])
        acc[...] -= product(split(x_near[3]), (tmp_hi[...], tmp_lo[...]))
        landed(a_far.at[0], far_sems.at[2])
        tmp_hi[...], tmp_lo[...] = transposed(a_far.at[0])
        left = split(flip[1, slot])
        landed(x_near.at[0], near_sems.at[0])
        acc[...] -= product(left, split(x_near[0]))
        landed(x_near.at[1], near_sems.at[1])
        acc[...] -= product(split(x_near[1]), (tmp_hi[...], tmp_lo[...]))
        solve()
    spread(2)

    for s in range(FRONTS):
        if s == FRONTS - 1:
            relay(s)
        for t in range(2):
            if s != 1:
                flip_wait(s, t, ~role[2] if s == 0 else every)
            leaf_wait(s, t)

            @pl.when(lags[t] >= FRONTS)
            def _():
                change = product(split(flip[s, t]), split(wide[s, t]))
                base = state[t] if s == 0 else out[t]
                out[t] = base - change
    for t in range(2):
        @pl.when(lags[t] < 0)
        def _():
            out[t] = state[t]

        @pl.when((lags[t] >= 0) & (lags[t] < FRONTS))
        def _():
            out[t] = own[...]
    posted.drain()


def per_device(nx, state, a_tiles, inverses):
    nc, nt = lax.axis_size("col"), lax.axis_size("row")
    order = inverses.shape[-1]
    tile = (order, order)
    in_vmem = pl.BlockSpec(memory_space=pltpu.VMEM)
    dma = pltpu.SemaphoreType.DMA
    result = pl.pallas_call(
        functools.partial(sweep, nt, nc, nx),
        out_shape=jax.ShapeDtypeStruct((2,) + tile, F32),
        in_specs=[in_vmem] * 3,
        out_specs=in_vmem,
        scratch_shapes=[
            pltpu.VMEM((FRONTS, 2) + tile, F32),
            pltpu.VMEM((FRONTS, 2) + tile, F32),
            pltpu.VMEM(tile, F32),
            pltpu.VMEM(tile, F32),
            pltpu.VMEM((2,) + tile, F32),
            pltpu.VMEM(tile, F32),
            pltpu.VMEM((4,) + tile, F32),
            pltpu.VMEM(tile, F32),
            pltpu.VMEM(tile, F32),
            pltpu.VMEM((DOUBLINGS,) + tile, BF16),
            pltpu.VMEM((DOUBLINGS,) + tile, BF16),
            pltpu.VMEM((DOUBLINGS,) + tile, BF16),
            pltpu.VMEM((DOUBLINGS,) + tile, BF16),
            pltpu.VMEM(tile, BF16),
            pltpu.VMEM(tile, BF16),
            dma((N_SENDS,)),
            dma((FRONTS, 2)),
            dma((FRONTS, 2, nx)),
            dma((5,)),
            dma((4,)),
            pltpu.SemaphoreType.REGULAR,
        ],
        compiler_params=pltpu.CompilerParams(collective_id=0, has_side_effects=True),
    )(state.reshape((2,) + tile), a_tiles.reshape((2,) + tile), inverses.reshape(tile))
    return result.reshape(state.shape)


def solution(mesh, nx=X_CHIPS):
    tiles = P("row", None, "col", None, None)
    return jax.shard_map(
        functools.partial(per_device, nx), mesh=mesh,
        in_specs=(tiles, tiles, P("row", None, None)), out_specs=tiles, check_vma=False,
    )
```
